128 devices in a mesh: sites: 8 (over x, core), rows: 16 (over z, y).
Axes of the slice: x: 4, y: 4, z: 4, core: 2. Of those that a mesh axis runs over, the one named last changes fastest.
Arguments:
- bond: bfloat16 [64, 384, 384], P('sites', 'rows')
- left_env: bfloat16 [64, 384, 5, 384], P('sites', 'rows'), as said below
- right_env: bfloat16 [64, 384, 5, 384], P('sites', 'rows'), as said below
Outputs:
- evolved: float32 [64, 384, 384], P('sites', 'rows')
Inputs may be any that keep to these rules, and one draw needn't show every extreme that they name: Each environment is symmetric in its two bond indices: left_env[b, k, a, i] = left_env[b, i, a, k]. Each environment is symmetric in its two bond indices: right_env[e, j, a, l] = right_env[e, l, a, j].
All inputs are finite; a program needn't handle non-finite values.
Results may differ from the reference program's by a relative error of at most 0.0049.
Values may be sent and summed in bfloat16 or wider, within the bound.
A program may use at most 64 MiB of HBM per device.

```python
import math
import jax
import jax.numpy as jnp
from jax import lax

CHI = 384
WM = 5
KRYLOV = 4
BONDS = 64


def symmetric_env(key, energy_slot, ident_slot):
    keys = jax.random.split(key, 3)
    shape = (BONDS, CHI, WM, CHI)
    base = jax.random.normal(keys[0], shape, jnp.float32)
    summed = (base + jnp.transpose(base, (0, 3, 2, 1))) * (2.0 * CHI) ** (-0.5)
    energies = jnp.exp(jax.random.uniform(keys[2], (BONDS, CHI, 1, 1), jnp.float32, math.log(0.05), math.log(4.0)))
    channel = jnp.arange(WM).reshape(1, 1, WM, 1)
    energy_mask = (channel == energy_slot).astype(jnp.float32)
    ident_mask = (channel == ident_slot).astype(jnp.float32)
    unit = jnp.eye(CHI, dtype=jnp.float32).reshape(1, CHI, 1, CHI)
    diagonal_part = unit * (energies * energy_mask + ident_mask)
    return (summed + diagonal_part).astype(jnp.bfloat16)


def draw_bond(key, part):
    keys = jax.random.split(jax.random.fold_in(key, 11), 3)
    row_scale = jnp.exp(jax.random.uniform(keys[1], (BONDS, CHI, 1), jnp.float32, math.log(0.3), math.log(3.0)))
    col_scale = jnp.exp(jax.random.uniform(keys[2], (BONDS, 1, CHI), jnp.float32, math.log(0.3), math.log(3.0)))
    base = jax.random.normal(keys[0], (BONDS, CHI, CHI), jnp.float32)
    return (0.5 * base * row_scale * col_scale).astype(jnp.bfloat16)


def draw_left_env(key, part):
    return symmetric_env(jax.random.fold_in(key, 23), WM - 1, 0)


def draw_right_env(key, part):
    return symmetric_env(jax.random.fold_in(key, 37), 0, WM - 1)


def setup_inputs(seed: int = 0) -> dict:
    splits = jax.random.split(jax.random.key(seed), 4)
    bond = draw_bond(jax.random.fold_in(splits[3], 71), 0)
    left_env = draw_left_env(jax.random.fold_in(splits[3], 71), 0)
    right_env = draw_right_env(jax.random.fold_in(splits[3], 71), 0)
    return dict(bond=bond, left_env=left_env, right_env=right_env)


small_eps = 1e-06
tau_step = 0.5
series_terms = 24

def krylov_weights(correlations, couplings):
    length = len(correlations)
    series_term = [jnp.ones_like(correlations[0])] + [jnp.zeros_like(correlations[0]) for _ in range(length - 1)]
    running = list(series_term)
    for order_n in range(1, series_terms + 1):
        fresh = []
        for row_idx in range(length):
            value = correlations[row_idx] * series_term[row_idx]
            if row_idx > 0:
                value = value + couplings[row_idx - 1] * series_term[row_idx - 1]
            if row_idx < length - 1:
                value = value + couplings[row_idx] * series_term[row_idx + 1]
            fresh.append(value * (tau_step / order_n))
        series_term = fresh
        running = [old + new for old, new in zip(running, series_term)]
    return running

def apply_operator(vector, left_one, right_one):
    rounded = lax.optimization_barrier(vector.astype(jnp.bfloat16)).astype(jnp.float32)
    crossed = jnp.einsum('kl,jal->kaj', rounded, right_one.astype(jnp.float32), precision=lax.Precision.HIGHEST)
    return jnp.einsum('kai,kaj->ij', left_one.astype(jnp.float32), crossed, precision=lax.Precision.HIGHEST)

def one_bond(inputs):
    bond_one, left_one, right_one = inputs
    start_matrix = bond_one.astype(jnp.float32)
    norm_now = jnp.sqrt(jnp.sum(start_matrix * start_matrix) + small_eps)
    vectors = [start_matrix / norm_now]
    correlations = []
    couplings = []
    previous = jnp.zeros_like(start_matrix)
    coupling_prev = jnp.float32(0.0)
    for lanczos_step in range(KRYLOV):
        current = vectors[lanczos_step]
        image = apply_operator(current, left_one, right_one)
        correlation_now = jnp.sum(current * image)
        correlations.append(correlation_now)
        if lanczos_step + 1 < KRYLOV:
            image = image - correlation_now * current - coupling_prev * previous
            coupling_now = jnp.sqrt(jnp.sum(image * image) + small_eps)
            couplings.append(coupling_now)
            previous = current
            coupling_prev = coupling_now
            vectors.append(image / coupling_now)
    weights = krylov_weights(correlations, couplings)
    combined = weights[0] * vectors[0]
    for index_k in range(1, KRYLOV):
        combined = combined + weights[index_k] * vectors[index_k]
    square_sum = weights[0] * weights[0]
    for index_k in range(1, KRYLOV):
        square_sum = square_sum + weights[index_k] * weights[index_k]
    return combined * (norm_now / jnp.sqrt(square_sum))

def reference(bond, left_env, right_env):
    shifted_env = jnp.roll(right_env, -1, axis=0)
    return lax.map(one_bond, (bond, left_env, shifted_env))
```

```python
import jax
import jax.numpy as jnp
from jax import lax
from jax.experimental import pallas as pl
from jax.experimental.pallas import tpu as pltpu
from jax.sharding import PartitionSpec as P

KRYLOV = 4
CHI = 384
WM = 5
eps = 1e-06
tau_step = 0.5
series_terms = 24


def krylov_weights(diag, off):
    length = len(diag)
    term = [jnp.ones_like(diag[0])] + [jnp.zeros_like(diag[0])] * (length - 1)
    running = list(term)
    for n in range(1, series_terms + 1):
        fresh = []
        for i in range(length):
            value = diag[i] * term[i]
            if i > 0:
                value = value + off[i - 1] * term[i - 1]
            if i < length - 1:
                value = value + off[i] * term[i + 1]
            fresh.append(value * (tau_step / n))
        term = fresh
        running = [old + new for old, new in zip(running, term)]
    return running


def total(x):
    return jnp.sum(jnp.sum(x, axis=0, keepdims=True), axis=1, keepdims=True)


def image_of(vec, left, right):
    rounded = vec.astype(jnp.bfloat16)
    image = None
    for a in range(WM):
        cols = slice(a * CHI, (a + 1) * CHI)
        crossed = jnp.dot(rounded, right[:, cols], preferred_element_type=jnp.float32)
        high = crossed.astype(jnp.bfloat16)
        low = (crossed - high.astype(jnp.float32)).astype(jnp.bfloat16)
        part = jnp.dot(left[:, cols], high, preferred_element_type=jnp.float32)
        part = part + jnp.dot(left[:, cols], low, preferred_element_type=jnp.float32)
        image = part if image is None else image + part
    return image


def lanczos(bond, left, right, vecs, out):
    start = bond[...].astype(jnp.float32)
    norm = jnp.sqrt(total(start * start) + eps)
    vecs[0] = start / norm
    diag, off = [], []
    for k in range(KRYLOV):
        image = image_of(vecs[k], left, right)
        alpha = total(vecs[k] * image)
        diag.append(alpha)
        if k + 1 < KRYLOV:
            w = image - alpha * vecs[k]
            if k > 0:
                w = w - off[k - 1] * vecs[k - 1]
            beta = jnp.sqrt(total(w * w) + eps)
            off.append(beta)
            vecs[k + 1] = w / beta
    weights = krylov_weights(diag, off)
    square = weights[0] * weights[0]
    for k in range(1, KRYLOV):
        square = square + weights[k] * weights[k]
    scale = norm / jnp.sqrt(square)
    combined = weights[0] * vecs[0]
    for k in range(1, KRYLOV):
        combined = combined + weights[k] * vecs[k]
    out[...] = combined * scale


def kernel(bond, left, right, out, vecs):
    lanczos(bond, left, right, vecs, out)


def swap(block):
    twice = jnp.repeat(block, 2, axis=0)
    got = lax.all_to_all(twice, "rows", 0, 0, tiled=True)
    return got.reshape(CHI, got.shape[-1])


def per_device(bond, left_env, right_env):
    n = bond.shape[0]
    size = lax.axis_size("sites")
    edge = lax.ppermute(right_env[:1], "sites", [((i + 1) % size, i) for i in range(size)])
    shifted = jnp.concatenate([right_env[1:], edge], axis=0)
    left = swap(left_env.reshape(n, -1, WM * CHI))
    right = swap(shifted.reshape(n, -1, WM * CHI))
    mine = swap(bond)
    out = pl.pallas_call(
        kernel,
        out_shape=jax.ShapeDtypeStruct((CHI, CHI), jnp.float32),
        scratch_shapes=[pltpu.VMEM((KRYLOV, CHI, CHI), jnp.float32)],
        compiler_params=pltpu.CompilerParams(vmem_limit_bytes=48 * 1024 * 1024),
    )(mine, left, right)
    ranks = lax.axis_size("rows")
    back = lax.all_to_all(out.reshape(ranks, -1, CHI), "rows", 0, 0, tiled=True)
    return back[::2]


def solution(mesh):
    placed = (
        P("sites", "rows", None),
        P("sites", "rows", None, None),
        P("sites", "rows", None, None),
    )
    return jax.shard_map(
        per_device, mesh=mesh, in_specs=placed, out_specs=P("sites", "rows", None), check_vma=False
    )
```
